32 devices in a mesh: row: 4 (over z), col: 8 (over y, x, core).
Axes of the slice: x: 2, y: 2, z: 4, core: 2. Of those that a mesh axis runs over, the one named last changes fastest.
Arguments:
- trial_factor: bfloat16 [2, 4096, 512], P(None, ('row', 'col')), may hold values from -6 to 6
- occupied: bfloat16 [4096, 512], P(('col', 'row')), may hold values from -0.25 to 0.25
- centers: float32 [3, 4096], P(None, ('row', 'col')), may hold values from 0 to 1
- exponents: float32 [4096], P(('row', 'col')), may hold values from 0.5 to 4
- wave_vectors: float32 [3, 4096], P(None, ('row', 'col')), may hold values from -36 to 36
- phases: float32 [4096], P(('row', 'col')), may hold values from -3.140625 to 3.140625
- points: float32 [64, 3, 1024], P(('row', 'col')), may hold values from 0 to 1
- density: float32 [64, 1024], P(('row', 'col')), may hold values from 0.05 to 1
- weights: float32 [64, 1024], P(('row', 'col')), may hold values from 0.0001 to 0.001
- sources: int32 [64, 8, 1], P(('row', 'col')), may hold values from 0 to 7; in each aligned block of 16 rows (0 to 15, 16 to 31, ..., all dimensions but the last counted through in order) at most 2 rows name the same one
Outputs:
- response: float32 [4096, 2, 512], P(('row', 'col'))
The draws below stay inside these ranges and needn't reach their ends.
Inputs may be any that keep to these rules, and one draw needn't show every extreme that they name: `sources`: among the 16 entries of the batches of one device, no column block is named more than 2 times, and some block exactly 2 times.
All inputs are finite; a program needn't handle non-finite values.
Results may differ from the reference program's by a relative error of at most 0.0065.
Values may be sent and summed in bfloat16 or wider, within the bound.
No kernel may reach another device: no remote copies, remote signals or barrier semaphores. Data moves between devices by JAX's collectives and lax.ppermute only.
A program may use at most 128 MiB of HBM per device.

```python
import math
import jax
import jax.numpy as jnp
import numpy as np
from jax import lax

NOCC = 512
TB = 256
TR = 4
TC = 2
K = 2
BATCH_DEV = 2
GB = 1024
NPAIR = 8
COLS = 8
NBF = 4096
BATCHES = 64
CAP = 2
N_COL = 8


def block_scale(stream_key, dims, split, smallest, top_value):
    gain = 1.0
    for axis_at, parts in split:
        steps = jax.random.uniform(jax.random.fold_in(jax.random.fold_in(stream_key, 6), axis_at), (parts,), jnp.float32, smallest / len(split), top_value / len(split))
        gain = gain * jnp.repeat(jnp.exp(steps), dims[axis_at] // parts).reshape((-1,) + (1,) * (len(dims) - 1 - axis_at))
    return gain


def routed_block(rng, own, number, rows, amount, top, bound, slope):
    ranking = jax.random.permutation(rng, amount)
    heavy_load, common = load_shares(amount, rows * top, bound, slope, True), load_shares(amount, rows * top, bound, slope, False)
    places = jnp.arange(amount)

    def named(lengths, rotation):
        used = int((lengths > 0).sum())
        fixed = max(1, used // 4)
        shifted = fixed + (places - fixed + rotation * (used - fixed)) % max(1, amount - fixed)
        return jnp.zeros((amount,), jnp.int32).at[ranking[jnp.where(places < fixed, places, shifted)]].set(jnp.asarray(lengths, jnp.int32))

    lengths = jnp.where(number % 4 == 0, named(heavy_load, number // 4), named(common, number - number // 4 - 1))
    mixed = jax.random.permutation(jax.random.fold_in(own, 3), amount)
    giver, sink = mixed[0:amount // 2 * 2:2], mixed[1:amount // 2 * 2:2]
    slack = jnp.minimum(lengths[giver] - 1, bound - lengths[sink]) // 2
    slack = jnp.where((giver == ranking[0]) | (sink == ranking[0]) | (lengths[sink] == 0), 0, jnp.maximum(slack, 0))
    shifted = jax.random.randint(jax.random.fold_in(own, 4), (amount // 2,), 0, 1 << 20) % (slack + 1)
    lengths = lengths.at[giver].add(-shifted).at[sink].add(shifted)
    members = jnp.searchsorted(jnp.cumsum(lengths), jnp.arange(rows * top), side="right").astype(jnp.int32)
    listing = members.reshape(top, rows).T
    listing = listing[jax.random.permutation(jax.random.fold_in(own, 1), rows)]
    rotation = jax.random.randint(jax.random.fold_in(own, 2), (rows, 1), 0, top)
    return jnp.take_along_axis(listing, (jnp.arange(top)[None, :] + rotation) % top, axis=1)


def load_shares(count, total, limit, lean, full):
    weights = [(1 << 20) // math.isqrt(standing ** lean) + 1 for standing in range(1, count + 1)]
    largest = limit if full else min(limit, max(-(-total // count), total * weights[0] // sum(weights)))
    least = 1 if total - largest >= count - 1 else 0
    given, rest = [largest] + [least] * (count - 1), total - largest - least * (count - 1)
    while rest > 0:
        free = [i for i in range(1, count) if given[i] < largest] or [i for i in range(1, count) if given[i] < limit]
        mass, left = sum([weights[i] for i in free]), rest
        for i in free:
            more = min(limit - given[i], max(1, left * weights[i] // mass), rest)
            given[i] = given[i] + more
            rest = rest - more
    return np.array(given)


def normal_values(own_key, dims, deviation, reach, shards=(), kind=jnp.bfloat16):
    gain = block_scale(own_key, dims, shards, -0.22, 0.18) if shards else 1.0
    entries = jax.random.normal(own_key, dims, jnp.float32) * deviation * gain
    return jnp.minimum(jnp.maximum(entries, -reach), reach).astype(kind)


def setup_inputs(seed: int = 0) -> dict:
    splits = jax.random.split(jax.random.key(seed), 11)
    trial_factor = normal_values(splits[0], (K, NBF, NOCC), 1.0, 6.0, ((1, 32),))
    occupied = normal_values(splits[1], (NBF, NOCC), NOCC ** -0.5, 0.25, ((0, 32),))
    centers = jnp.clip(1.0 * jax.random.uniform(splits[2], (3, NBF), jnp.float32) ** block_scale(splits[2], (3, NBF), ((1, 32),), -0.2, 0.2), 0.0, 1.0)
    exponents = jnp.clip(jnp.exp(math.log(4.0) - 2.0794415 * jax.random.uniform(splits[3], (NBF,), jnp.float32) ** block_scale(splits[3], (NBF,), ((0, 32),), -0.2, 0.2)), 0.5, 4.0)
    wave_vectors = normal_values(splits[4], (3, NBF), 6.0, 36.0, ((1, 32),), jnp.float32)
    phases = jnp.clip(jax.random.uniform(splits[5], (NBF,), jnp.float32, -3.140625, 3.140625), -3.140625, 3.140625)
    points = jnp.clip(1.0 * jax.random.uniform(splits[6], (BATCHES, 3, GB), jnp.float32) ** block_scale(splits[6], (BATCHES, 3, GB), ((0, 32),), -0.2, 0.2), 0.0, 1.0)
    density = jnp.clip(jnp.exp(math.log(1.0) - 2.9957323 * jax.random.uniform(splits[7], (BATCHES, GB), jnp.float32) ** block_scale(splits[7], (BATCHES, GB), ((0, 32),), -0.2, 0.2)), 0.05, 1.0)
    weights = jnp.clip(jnp.exp(math.log(0.001) - 2.3025852 * jax.random.uniform(splits[8], (BATCHES, GB), jnp.float32) ** block_scale(splits[8], (BATCHES, GB), ((0, 32),), -0.2, 0.2)), 0.0001, 0.001)
    sources_keys = jax.random.split(jax.random.fold_in(splits[9], 1), BATCHES * NPAIR // (BATCH_DEV * NPAIR))
    sources_turns = jax.random.permutation(jax.random.fold_in(splits[9], 3), BATCHES * NPAIR // (BATCH_DEV * NPAIR))
    sources = jax.vmap(lambda own, number: routed_block(jax.random.fold_in(splits[9], 2), own, number, BATCH_DEV * NPAIR, COLS, 1, CAP, 2))(sources_keys, sources_turns).reshape((BATCHES, NPAIR, 1))
    return dict(trial_factor=trial_factor, occupied=occupied, centers=centers, exponents=exponents, wave_vectors=wave_vectors, phases=phases, points=points, density=density, weights=weights, sources=sources)


EXCHANGE_COEF = 0.75 * (3.0 / 3.141592653589793) ** (1.0 / 3.0)


def collocate(grid_points, func_centers, func_exponents, func_waves, func_phases):
    npoints = grid_points.shape[1]
    nfuncs = func_centers.shape[1]
    radius = jnp.zeros((npoints, nfuncs), jnp.float32)
    phase_sum = jnp.zeros((npoints, nfuncs), jnp.float32) + func_phases[None, :]
    for coordinate in range(3):
        offset = grid_points[coordinate][:, None] - func_centers[coordinate][None, :]
        radius = radius + offset * offset
        phase_sum = phase_sum + grid_points[coordinate][:, None] * func_waves[coordinate][None, :]
    return (jnp.exp(-func_exponents[None, :] * radius) * jnp.cos(phase_sum)).astype(jnp.bfloat16)


def batch_response(ground, quad_weights, row_values, col_values, pair_tiles):
    npoints = col_values.shape[0]
    row_tiles = pair_tiles.shape[0]
    col_span = pair_tiles.shape[1]
    tile_width = pair_tiles.shape[2]
    tile_size = row_values.shape[1] // row_tiles
    vectors = tile_width // tile_size
    col_phi = col_values.reshape(npoints, row_tiles, col_span).astype(jnp.float32)
    half_contracted = jnp.einsum('gax,axy->gay', col_phi, pair_tiles.astype(jnp.float32), precision=lax.Precision.HIGHEST)
    half_contracted = half_contracted.reshape(npoints, row_tiles, vectors, tile_size)
    row_phi = row_values.astype(jnp.float32).reshape(npoints, row_tiles, 1, tile_size)
    response_density = jnp.sum(half_contracted * row_phi, axis=(1, 3))
    kernel = -(4.0 / 9.0) * EXCHANGE_COEF * jnp.exp(-(2.0 / 3.0) * jnp.log(ground))
    potential = (quad_weights * kernel)[:, None] * response_density
    scaled = (potential[:, None, :, None] * row_phi).astype(jnp.bfloat16).reshape(npoints, row_tiles, tile_width)
    matrix = jnp.einsum('gax,gay->axy', col_phi, scaled.astype(jnp.float32), precision=lax.Precision.HIGHEST)
    return matrix.astype(jnp.bfloat16)


def reference(trial_factor, occupied, centers, exponents, wave_vectors, phases, points, density, weights, sources):
    span_row = TR * TB
    orbital_count = occupied.shape[1]
    tile_offsets = jnp.arange(TB, dtype=jnp.int32)
    pair_slots = jnp.arange(NPAIR, dtype=jnp.int32)

    def one_batch(position, response):
        position = jnp.asarray(position).astype(jnp.int32)
        row_block = (position // BATCH_DEV) // N_COL
        row_start = (row_block * span_row).astype(jnp.int32)
        row_factor = lax.dynamic_slice_in_dim(trial_factor, row_start, span_row, 1)
        column_tile = sources[position, :, 0] * TC + pair_slots % TC
        column_index = (column_tile[:, None] * TB + tile_offsets[None, :]).reshape(NPAIR * TB).astype(jnp.int32)
        factor_rows = jnp.take(occupied, column_index, axis=0).reshape(TR, TC, TB, orbital_count)
        pair_tiles = jnp.einsum('kami,abni->abnkm', row_factor.astype(jnp.float32).reshape(K, TR, TB, orbital_count), factor_rows.astype(jnp.float32), precision=lax.Precision.HIGHEST)
        pair_tiles = pair_tiles.astype(jnp.bfloat16).reshape(TR, TC * TB, K * TB)
        grid_points = points[position]
        row_values = collocate(grid_points, lax.dynamic_slice_in_dim(centers, row_start, span_row, 1), lax.dynamic_slice_in_dim(exponents, row_start, span_row, 0), lax.dynamic_slice_in_dim(wave_vectors, row_start, span_row, 1), lax.dynamic_slice_in_dim(phases, row_start, span_row, 0))
        col_values = collocate(grid_points, jnp.take(centers, column_index, axis=1), jnp.take(exponents, column_index), jnp.take(wave_vectors, column_index, axis=1), jnp.take(phases, column_index))
        pair_potential = batch_response(density[position], weights[position], row_values, col_values, pair_tiles)
        contrib = jnp.einsum('axkm,axi->amki', pair_potential.astype(jnp.float32).reshape(TR, TC * TB, K, TB), factor_rows.reshape(TR, TC * TB, orbital_count).astype(jnp.float32), precision=lax.Precision.HIGHEST)
        current = lax.dynamic_slice_in_dim(response, row_start, span_row, 0)
        return lax.dynamic_update_slice_in_dim(response, current + contrib.reshape(span_row, K, orbital_count), row_start, 0)

    start_value = jnp.zeros((NBF, K, orbital_count), jnp.float32)
    return lax.fori_loop(0, BATCHES, one_batch, start_value)
```

```python
import math

import jax
import jax.numpy as jnp
from jax import lax
from jax.experimental import pallas as pl
from jax.experimental.pallas import tpu as pltpu
from jax.sharding import PartitionSpec as P

TB = 256

EXCHANGE_COEF = 0.75 * (3.0 / 3.141592653589793) ** (1.0 / 3.0)
LOG2E = 1.4426950408889634
INV_TURN = 0.15915494309189535
SHIFT = 0.5
FEATURES = 16
KDIM = 128
PARAM_ROWS = 8
ROUNDER = 12582912.0
RING = (0, 3, 1, 2)


def sine_coefficients():
    terms = 4
    nodes = 64
    xs = [0.5 * (0.25 + 0.25 * math.cos(math.pi * (i + 0.5) / nodes) * 1.0) * 2.0 * 0.5 for i in range(nodes)]
    rows = [[0.0] * (terms + 1) for _ in range(terms)]
    for s in xs:
        r = math.sqrt(s)
        value = math.sqrt(2.0) * (math.sin(math.pi * r) / r)
        for i in range(terms):
            for j in range(terms):
                rows[i][j] += s ** (i + j)
            rows[i][terms] += value * s**i
    for i in range(terms):
        pivot = rows[i][i]
        rows[i] = [v / pivot for v in rows[i]]
        for j in range(terms):
            if j != i:
                factor = rows[j][i]
                rows[j] = [a - factor * b for a, b in zip(rows[j], rows[i])]
    return [rows[i][terms] for i in range(terms)]


SINE = sine_coefficients()


def split3(value):
    first = value.astype(jnp.bfloat16).astype(jnp.float32)
    rest = value - first
    second = rest.astype(jnp.bfloat16).astype(jnp.float32)
    third = (rest - second).astype(jnp.bfloat16).astype(jnp.float32)
    return first, second, third


def prep_kernel(occ, centers, expo, waves, phases, points, density, weights, sources, payload, feats, raw, stage, fstage):
    raw[0:3, :] = centers[...]
    raw[3:6, :] = waves[...]
    raw[6:7, :] = expo[...]
    raw[7:8, :] = phases[...]
    pieces = split3(raw[...])
    lanes = raw.shape[1]
    payload[0 : occ.shape[0], :] = occ[...]
    stage[...] = jnp.zeros(stage.shape, jnp.float32)
    per_row = stage.shape[1] // lanes
    for piece in range(3):
        for row in range(8):
            flat = piece * 8 + row
            stage[flat // per_row : flat // per_row + 1, (flat % per_row) * lanes : (flat % per_row + 1) * lanes] = pieces[piece][row : row + 1, :]
    payload[occ.shape[0] : occ.shape[0] + PARAM_ROWS, :] = stage[...].astype(jnp.bfloat16)
    npoints = points.shape[2]
    for i in range(points.shape[0]):
        local = points[i] - SHIFT
        square = jnp.sum(local * local, axis=0, keepdims=True)
        ground = density[i : i + 1, :]
        kernel = -(4.0 / 9.0) * EXCHANGE_COEF * jnp.exp(-(2.0 / 3.0) * jnp.log(ground))
        factor = split3(weights[i : i + 1, :] * kernel)
        lp = split3(local)
        sq = split3(square)
        fstage[...] = jnp.zeros(fstage.shape, jnp.float32)
        for piece in range(3):
            fstage[4 * piece : 4 * piece + 3, 0:npoints] = lp[piece]
            fstage[4 * piece + 3 : 4 * piece + 4, 0:npoints] = sq[piece]
            fstage[13 + piece : 14 + piece, 0:npoints] = factor[piece]
        fstage[12:13, 0:npoints] = jnp.ones((1, npoints), jnp.float32)
        fstage[0:1, npoints : npoints + 128] = sources[i : i + 1, :]
        feats[i] = fstage[...].astype(jnp.bfloat16)


def build_args(values, stage):
    c = [values[d : d + 1, :] - SHIFT for d in range(3)]
    k = [values[3 + d : 4 + d, :] for d in range(3)]
    alpha = values[6:7, :] * LOG2E
    phi = values[7:8, :]
    tile = values.shape[1]
    exp_rows = [2.0 * alpha * c[d] for d in range(3)] + [-alpha, -alpha * (c[0] * c[0] + c[1] * c[1] + c[2] * c[2])]
    phase_rows = [k[d] * INV_TURN for d in range(3)] + [jnp.zeros_like(alpha), (phi + SHIFT * (k[0] + k[1] + k[2])) * INV_TURN]
    stage[...] = jnp.zeros(stage.shape, jnp.float32)
    for part, rows in ((0, exp_rows), (1, phase_rows)):
        lanes = slice(part * tile, (part + 1) * tile)
        for row, coefficient in enumerate(rows):
            pieces = split3(coefficient)
            for piece in range(3):
                base = FEATURES * piece
                if row < 4:
                    for copy in range(3):
                        stage[base + 4 * copy + row : base + 4 * copy + row + 1, lanes] = pieces[piece]
                else:
                    stage[base + 12 : base + 13, lanes] = pieces[piece]
    return jnp.transpose(stage[...], (1, 0)).astype(jnp.bfloat16)


def spread(block):
    zeros = jnp.zeros((KDIM - 3 * FEATURES, block.shape[1]), jnp.bfloat16)
    return jnp.concatenate([block, block, block, zeros], axis=0)


def collocate_tile(coefficients, block):
    args = jnp.dot(coefficients, spread(block), preferred_element_type=jnp.float32)
    tile = args.shape[0] // 2
    turns = args[tile:]
    r = turns - ((turns + ROUNDER) - ROUNDER)
    s = r * r
    poly = SINE[3]
    for coefficient in (SINE[2], SINE[1], SINE[0]):
        poly = poly * s + coefficient
    y = r * poly
    return (jnp.exp2(args[:tile]) * (1.0 - y * y)).astype(jnp.bfloat16)


def join_raw(own, other, odd):
    lower = jnp.where(odd, other, own)
    upper = jnp.where(odd, own, other)
    return jnp.concatenate([lower, upper], axis=1)


def row_kernel(pos, raw_own, raw_other, feat_own, feat_other, phi, feat, src, coeff, stage):
    step = pl.program_id(0)
    odd = pos[1] % 2

    @pl.when(step == 0)
    def _():
        coeff[...] = build_args(join_raw(raw_own[...], raw_other[...], odd == 1), stage)

    mine = ((step // 2) % 2) == odd
    block = jnp.where(mine, feat_own[0, 0], feat_other[0, 0])
    feat[0] = block
    npoints = phi.shape[2]
    src[0] = block[0:1, npoints:].astype(jnp.float32).astype(jnp.int32)
    width = 256
    for start in range(0, npoints, width):
        phi[0, :, start : start + width] = collocate_tile(coeff[...], block[:, start : start + width])


def column_kernel(meta, *refs):
    (slots, where_block, n_arrays) = meta
    arrays = refs[:n_arrays]
    (src, x_own, x_other, phi_a, feat, phi_b, rho, occ_out) = refs[n_arrays : n_arrays + 8]
    (occ, par, tiles, coeff, trial, stage, sem_c, sem_p, sem_o) = refs[n_arrays + 8 :]
    step = pl.program_id(0)
    column = lax.axis_index("col")
    odd = column % 2
    quarter = occ.shape[1] // 2
    blocks = occ.shape[0]

    @pl.when(step == 0)
    def _():
        jobs = []
        for index, (which, slot, name) in enumerate(slots):
            (c_ok, c_block, c_half), (p_ok, p_block, p_half) = where_block(name)
            base = c_half * quarter
            if not isinstance(base, int):
                base = pl.multiple_of(base, quarter)
            copy_c = pltpu.make_async_copy(arrays[which].at[slot, 0:quarter], occ.at[c_block, pl.ds(base, quarter)], sem_c.at[index])
            copy_p = pltpu.make_async_copy(arrays[which].at[slot, quarter : quarter + PARAM_ROWS], par.at[p_block, p_half], sem_p.at[index])
            jobs.append((c_ok, copy_c, p_ok, copy_p))
        for c_ok, copy_c, p_ok, copy_p in jobs:
            pl.when(c_ok)(copy_c.start)
            pl.when(p_ok)(copy_p.start)
        half = x_own.shape[1]
        for k in range(x_own.shape[0]):
            for part, ref in ((odd, x_own), (1 - odd, x_other)):
                trial[pl.ds(pl.multiple_of(k * 2 * half + part * half, half), half), :] = ref[k]
        for c_ok, copy_c, p_ok, copy_p in jobs:
            pl.when(c_ok)(copy_c.wait)
            pl.when(p_ok)(copy_p.wait)
        pltpu.make_async_copy(occ, occ_out, sem_o).start()

        def prepare(b, carry):
            halves = []
            for h in range(2):
                packed = par[b, h].astype(jnp.float32)
                lanes = quarter
                per_row = packed.shape[1] // lanes
                total = None
                for piece in range(3):
                    rows = []
                    for row in range(8):
                        flat = piece * 8 + row
                        rows.append(packed[flat // per_row : flat // per_row + 1, (flat % per_row) * lanes : (flat % per_row + 1) * lanes])
                    part = jnp.concatenate(rows, axis=0)
                    total = part if total is None else total + part
                halves.append(total)
            coeff[b] = build_args(jnp.concatenate(halves, axis=1), stage)
            tiles[b] = lax.dot_general(trial[...], occ[b], (((1,), (1,)), ((), ())), preferred_element_type=jnp.float32).astype(jnp.bfloat16)
            return carry

        lax.fori_loop(0, blocks, prepare, 0)
        pltpu.make_async_copy(occ, occ_out, sem_o).wait()

    block = src[step, column]
    npoints = phi_b.shape[2]
    tile = phi_a.shape[1]
    width = 256
    for start in range(0, npoints, width):
        lanes = slice(start, start + width)
        values = collocate_tile(coeff[block], feat[0, :, lanes])
        phi_b[0, :, lanes] = values
        half_contracted = jnp.dot(tiles[block], values, preferred_element_type=jnp.float32)
        row_phi = phi_a[0, :, lanes].astype(jnp.float32)
        for k in range(rho.shape[1]):
            rho[0, k : k + 1, lanes] = jnp.sum(half_contracted[k * tile : (k + 1) * tile] * row_phi, axis=0, keepdims=True)


def potential_kernel(src, rho, phi_a, phi_b, feat, occ, keep, send, summed):
    step = pl.program_id(0)
    column = lax.axis_index("col")
    odd = column % 2

    @pl.when(step == 0)
    def _():
        summed[...] = jnp.zeros(summed.shape, jnp.float32)

    block = src[step, column]
    npoints = phi_b.shape[2]
    factor = (feat[0, 13:14, 0:npoints].astype(jnp.float32) + feat[0, 14:15, 0:npoints].astype(jnp.float32)) + feat[0, 15:16, 0:npoints].astype(jnp.float32)
    row_phi = phi_a[0].astype(jnp.float32)
    scaled = jnp.concatenate([(row_phi * (factor * rho[0, k : k + 1, :])).astype(jnp.bfloat16) for k in range(rho.shape[1])], axis=0)
    matrix = lax.dot_general(scaled, phi_b[0], (((1,), (1,)), ((), ())), preferred_element_type=jnp.float32)
    summed[block] = summed[block] + matrix

    @pl.when(step == pl.num_programs(0) - 1)
    def _():
        vectors = rho.shape[1]
        tile = phi_a.shape[1]
        part = tile // 2
        total = None
        for b in range(summed.shape[0]):
            piece = jnp.dot(summed[b].astype(jnp.bfloat16), occ[b], preferred_element_type=jnp.float32)
            total = piece if total is None else total + piece
        for k in range(vectors):
            lower = total[k * tile : k * tile + part]
            upper = total[k * tile + part : (k + 1) * tile]
            keep[k] = jnp.where(odd == 1, upper, lower)
            send[k] = jnp.where(odd == 1, lower, upper)


def collocate(grid_points, func_centers, func_exponents, func_waves, func_phases):
    npoints = grid_points.shape[1]
    nfuncs = func_centers.shape[1]
    radius = jnp.zeros((npoints, nfuncs), jnp.float32)
    phase_sum = jnp.zeros((npoints, nfuncs), jnp.float32) + func_phases[None, :]
    for coordinate in range(3):
        offset = grid_points[coordinate][:, None] - func_centers[coordinate][None, :]
        radius = radius + offset * offset
        phase_sum = phase_sum + grid_points[coordinate][:, None] * func_waves[coordinate][None, :]
    return (jnp.exp(-func_exponents[None, :] * radius) * jnp.cos(phase_sum)).astype(jnp.bfloat16)


def batch_response(ground, quad_weights, row_values, col_values, pair_tiles):
    npoints = col_values.shape[0]
    row_tiles = pair_tiles.shape[0]
    col_span = pair_tiles.shape[1]
    tile_width = pair_tiles.shape[2]
    tile_size = row_values.shape[1] // row_tiles
    vectors = tile_width // tile_size
    col_phi = col_values.reshape(npoints, row_tiles, col_span)
    half_contracted = jnp.einsum(
        "gax,axy->gay", col_phi, pair_tiles, preferred_element_type=jnp.float32
    )
    half_contracted = half_contracted.reshape(npoints, row_tiles, vectors, tile_size)
    row_phi = row_values.astype(jnp.float32).reshape(npoints, row_tiles, 1, tile_size)
    response_density = jnp.sum(half_contracted * row_phi, axis=(1, 3))
    kernel = -(4.0 / 9.0) * EXCHANGE_COEF * jnp.exp(-(2.0 / 3.0) * jnp.log(ground))
    potential = (quad_weights * kernel)[:, None] * response_density
    scaled = (
        (potential[:, None, :, None] * row_phi)
        .astype(jnp.bfloat16)
        .reshape(npoints, row_tiles, tile_width)
    )
    matrix = jnp.einsum("gax,gay->axy", col_phi, scaled, preferred_element_type=jnp.float32)
    return matrix.astype(jnp.bfloat16)


def general_device(
    trial_factor,
    occupied,
    centers,
    exponents,
    wave_vectors,
    phases,
    points,
    density,
    weights,
    sources,
):
    columns = lax.axis_size("col")
    row_block = lax.axis_index("row")
    all_centers, all_waves, all_exponents, all_phases = (
        lax.all_gather(centers, ("row", "col"), axis=1, tiled=True),
        lax.all_gather(wave_vectors, ("row", "col"), axis=1, tiled=True),
        lax.all_gather(exponents, ("row", "col"), axis=0, tiled=True),
        lax.all_gather(phases, ("row", "col"), axis=0, tiled=True),
    )
    col_factor = lax.all_gather(occupied, "row", axis=0, tiled=True)
    span_col = col_factor.shape[0]
    orbital_count = col_factor.shape[1]
    tiles_col = span_col // TB
    span_row = trial_factor.shape[1] * columns
    tiles_row = span_row // TB
    vectors = trial_factor.shape[0]
    pair_count = tiles_row * tiles_col
    batch_count = sources.shape[0]
    slot_count = batch_count * pair_count
    slot_source = sources.reshape(slot_count)
    capacity = max(2, (slot_count + columns - 1) // columns)
    source_hot = (slot_source[:, None] == jnp.arange(columns, dtype=jnp.int32)[None, :]).astype(
        jnp.int32
    )
    slot_rank = jnp.sum(source_hot * (jnp.cumsum(source_hot, axis=0) - 1), axis=1)
    slot_place = slot_source * capacity + slot_rank
    slot_pair = jnp.arange(slot_count, dtype=jnp.int32) % pair_count
    place_hot = slot_place[:, None] == jnp.arange(columns * capacity, dtype=jnp.int32)[None, :]
    place_matrix = place_hot.astype(jnp.bfloat16)
    wanted = jnp.sum(place_hot.astype(jnp.int32) * (slot_pair[:, None] + 1), axis=0) - 1
    asked_pairs = lax.all_to_all(
        wanted.reshape(columns, capacity), "col", split_axis=0, concat_axis=0, tiled=True
    )
    asked_flat = asked_pairs.reshape(columns * capacity)
    asked_col = jnp.where(asked_flat >= 0, asked_flat % tiles_col, -1)
    col_hot = (asked_col[:, None] == jnp.arange(tiles_col, dtype=jnp.int32)[None, :]).astype(
        jnp.bfloat16
    )
    row_start = row_block * span_row
    row_centers = lax.dynamic_slice_in_dim(all_centers, row_start, span_row, 1)
    row_waves = lax.dynamic_slice_in_dim(all_waves, row_start, span_row, 1)
    row_exponents = lax.dynamic_slice_in_dim(all_exponents, row_start, span_row, 0)
    row_phases = lax.dynamic_slice_in_dim(all_phases, row_start, span_row, 0)
    tile_offsets = jnp.arange(TB, dtype=jnp.int32)
    column_tile = slot_source * tiles_col + slot_pair % tiles_col
    column_index = (column_tile[:, None] * TB + tile_offsets[None, :]).reshape(
        batch_count, pair_count * TB
    )
    row_trial = lax.all_gather(trial_factor, "col", axis=1, tiled=True)
    row_split = row_trial.reshape(vectors, tiles_row, TB, orbital_count)
    outgoing_rows = (
        jnp.dot(
            col_hot,
            col_factor.reshape(tiles_col, TB * orbital_count),
            preferred_element_type=jnp.float32,
        )
        .astype(jnp.bfloat16)
        .reshape(columns, capacity, TB * orbital_count)
    )
    incoming_rows = lax.all_to_all(outgoing_rows, "col", split_axis=0, concat_axis=0, tiled=True)
    slot_rows = jnp.dot(
        place_matrix,
        incoming_rows.reshape(columns * capacity, TB * orbital_count),
        preferred_element_type=jnp.float32,
    ).astype(jnp.bfloat16)
    slot_rows = slot_rows.reshape(batch_count, tiles_row, tiles_col * TB, orbital_count)
    accumulated = jnp.zeros((span_row, vectors, orbital_count), jnp.float32)
    for position in range(batch_count):
        factor_rows = slot_rows[position]
        tiles_now = (
            jnp.einsum("kami,axi->axkm", row_split, factor_rows, preferred_element_type=jnp.float32)
            .astype(jnp.bfloat16)
            .reshape(tiles_row, tiles_col * TB, vectors * TB)
        )
        index_now = column_index[position]
        row_values = collocate(points[position], row_centers, row_exponents, row_waves, row_phases)
        col_values = collocate(
            points[position],
            jnp.take(all_centers, index_now, axis=1),
            jnp.take(all_exponents, index_now),
            jnp.take(all_waves, index_now, axis=1),
            jnp.take(all_phases, index_now),
        )
        potential_now = batch_response(
            density[position], weights[position], row_values, col_values, tiles_now
        )
        contrib = jnp.einsum(
            "axkm,axi->amki",
            potential_now.reshape(tiles_row, tiles_col * TB, vectors, TB),
            factor_rows,
            preferred_element_type=jnp.float32,
        )
        accumulated = accumulated + contrib.reshape(span_row, vectors, orbital_count)
    return lax.psum_scatter(accumulated, "col", scatter_dimension=0, tiled=True)


def fast_device(n_row, n_col):
    chips = n_col // 2
    pairs_core = [(c, c ^ 1) for c in range(n_col)]

    def xy(bits):
        return [(c, c ^ (2 * bits)) for c in range(n_col)]

    def world(z_move, xy_bits, plane_core):
        out = []
        for z in range(n_row):
            for c in range(n_col):
                if c % 2 == plane_core:
                    out.append((z * n_col + c, z * n_col + (c ^ (2 * xy_bits))))
                else:
                    out.append((z * n_col + c, ((z + z_move) % n_row) * n_col + c))
        return out

    both = ("row", "col")

    def per_device(trial_factor, occupied, centers, exponents, wave_vectors, phases, points, density, weights, sources):
        row = lax.axis_index("row")
        column = lax.axis_index("col")
        pos = jnp.stack([row, column]).astype(jnp.int32)
        batches, _, npoints = points.shape
        quarter, orbitals = occupied.shape
        vectors = trial_factor.shape[0]
        slots = sources.shape[1]
        total = batches * n_col
        wide = npoints + 128
        source_row = jnp.pad(sources.reshape(batches, slots).astype(jnp.float32), ((0, 0), (0, 128 - slots)))
        payload, feats, raw = pl.pallas_call(
            prep_kernel,
            out_shape=(
                jax.ShapeDtypeStruct((quarter + PARAM_ROWS, orbitals), jnp.bfloat16),
                jax.ShapeDtypeStruct((batches, FEATURES, wide), jnp.bfloat16),
                jax.ShapeDtypeStruct((8, quarter), jnp.float32),
            ),
            scratch_shapes=[pltpu.VMEM((PARAM_ROWS, orbitals), jnp.float32), pltpu.VMEM((FEATURES, wide), jnp.float32)],
            name="prep",
        )(occupied, centers, exponents.reshape(1, -1), wave_vectors, phases.reshape(1, -1), points, density, weights, source_row)

        raw_other = lax.ppermute(raw, "col", pairs_core)
        fx = lax.ppermute(feats, "col", xy(1))
        fy = lax.ppermute(feats, "col", xy(2))
        fd = lax.ppermute(feats, "col", xy(3))
        s1 = [payload]
        for z_move, bits in ((1, 1), (-1, 2), (2, 3)):
            s1.append(lax.ppermute(payload, both, world(z_move, bits, 1)))
        x_other = lax.ppermute(trial_factor, "col", pairs_core)
        feat_own = jnp.stack([feats, fx, fy, fd])
        feat_other = lax.ppermute(feat_own, "col", pairs_core)
        n0 = jnp.stack(s1)
        r1 = lax.ppermute(n0, both, world(1, 1, 0))
        r2 = lax.ppermute(n0, both, world(-1, 2, 0))
        d1 = lax.ppermute(r1[0:2], both, world(1, 2, 0))
        d2 = lax.ppermute(r2[2:4], both, world(-1, 1, 0))
        own_net = [n0, r1, r2, d1, d2]
        other_net = [lax.ppermute(a, "col", pairs_core) for a in own_net]

        full = lambda shape: pl.BlockSpec(shape, lambda t, *_: (0,) * len(shape))
        per_batch = lambda shape: pl.BlockSpec((1,) + shape, lambda t, *_: (t, 0, 0))
        feat_spec = pl.BlockSpec((1, 1, FEATURES, wide), lambda t, pos: ((t // 4) ^ (pos[1] // 2), t % 2, 0, 0))
        phi_a, feat, src = pl.pallas_call(
            row_kernel,
            grid_spec=pltpu.PrefetchScalarGridSpec(
                num_scalar_prefetch=1,
                grid=(total,),
                in_specs=[full((8, quarter)), full((8, quarter)), feat_spec, feat_spec],
                out_specs=[per_batch((TB, npoints)), per_batch((FEATURES, wide)), per_batch((1, 128))],
                scratch_shapes=[pltpu.VMEM((2 * TB, KDIM), jnp.bfloat16), pltpu.VMEM((KDIM, 2 * TB), jnp.float32)],
            ),
            out_shape=(
                jax.ShapeDtypeStruct((total, TB, npoints), jnp.bfloat16),
                jax.ShapeDtypeStruct((total, FEATURES, wide), jnp.bfloat16),
                jax.ShapeDtypeStruct((total, 1, 128), jnp.int32),
            ),
            name="row_collocation",
        )(pos, raw, raw_other, feat_own, feat_other)
        src = src.reshape(total, 128)

        names = []
        for net in range(2):
            for which, (slot2, first, count) in enumerate(((0, 0, 4), (1, 0, 4), (2, 0, 4), (3, 0, 2), (3, 2, 2))):
                for slot in range(count):
                    names.append((net * 5 + which, slot, (net, slot2, first + slot)))

        def where_block(name):
            net, slot2, slot1 = name
            z = lax.axis_index("row")
            c = lax.axis_index("col")
            chip, core = c // 2, c % 2
            kind = core if net == 0 else 1 - core
            first = kind == 0
            zz = jnp.where(first, (z + RING[slot1]) % n_row, (z + RING[slot2]) % n_row)
            cc = jnp.where(first, chip ^ slot2, chip ^ slot1)
            owner = 2 * cc + kind
            per_tile = TB // quarter
            unit = zz * n_col + owner
            per_block = n_row
            c_info = (zz // per_tile == core, owner, zz % per_tile)
            p_info = ((unit % per_block) // per_tile == core, unit // per_block, unit % per_tile)
            return c_info, p_info

        anyspec = pl.BlockSpec(memory_space=pl.ANY)
        smem = pl.BlockSpec(memory_space=pltpu.SMEM)
        arrays = own_net + other_net
        phi_b, rho, occ = pl.pallas_call(
            lambda *refs: column_kernel((names, where_block, len(arrays)), *refs),
            grid=(total,),
            in_specs=[anyspec] * len(arrays)
            + [smem, full(trial_factor.shape), full(trial_factor.shape), per_batch((TB, npoints)), per_batch((FEATURES, wide))],
            out_specs=[per_batch((TB, npoints)), per_batch((vectors, npoints)), anyspec],
            out_shape=(
                jax.ShapeDtypeStruct((total, TB, npoints), jnp.bfloat16),
                jax.ShapeDtypeStruct((total, vectors, npoints), jnp.float32),
                jax.ShapeDtypeStruct((n_col, TB, orbitals), jnp.bfloat16),
            ),
            scratch_shapes=[
                pltpu.VMEM((n_col, TB, orbitals), jnp.bfloat16),
                pltpu.VMEM((n_col, 2, PARAM_ROWS, orbitals), jnp.bfloat16),
                pltpu.VMEM((n_col, vectors * TB, TB), jnp.bfloat16),
                pltpu.VMEM((n_col, 2 * TB, KDIM), jnp.bfloat16),
                pltpu.VMEM((vectors * TB, orbitals), jnp.bfloat16),
                pltpu.VMEM((KDIM, 2 * TB), jnp.float32),
                pltpu.SemaphoreType.DMA((len(names),)),
                pltpu.SemaphoreType.DMA((len(names),)),
                pltpu.SemaphoreType.DMA,
            ],
            name="column_density",
        )(*arrays, src, trial_factor, x_other, phi_a, feat)

        rho = rho + lax.ppermute(rho, "col", pairs_core)
        rx = lax.ppermute(rho, "col", xy(1))
        ry = lax.ppermute(rho, "col", xy(2))
        rd = lax.ppermute(rho, "col", xy(3))
        rho = (rho + rx) + (ry + rd)

        part = (vectors, TB // 2, orbitals)
        keep, send = pl.pallas_call(
            potential_kernel,
            grid=(total,),
            in_specs=[smem, per_batch((vectors, npoints)), per_batch((TB, npoints)), per_batch((TB, npoints)), per_batch((FEATURES, wide)), full((n_col, TB, orbitals))],
            out_specs=[full(part), full(part)],
            out_shape=(jax.ShapeDtypeStruct(part, jnp.float32), jax.ShapeDtypeStruct(part, jnp.float32)),
            scratch_shapes=[pltpu.VMEM((n_col, vectors * TB, TB), jnp.float32)],
            name="response",
        )(src, rho, phi_a, phi_b, feat, occ)
        result = keep + lax.ppermute(send, "col", pairs_core)
        return jnp.transpose(result, (1, 0, 2))

    return per_device


def solution(mesh):
    n_row, n_col = mesh.shape["row"], mesh.shape["col"]
    in_specs = (
        P(None, ("row", "col"), None),
        P(("col", "row"), None),
        P(None, ("row", "col")),
        P(("row", "col")),
        P(None, ("row", "col")),
        P(("row", "col")),
        P(("row", "col"), None, None),
        P(("row", "col"), None),
        P(("row", "col"), None),
        P(("row", "col"), None, None),
    )
    out_specs = P(("row", "col"), None, None)
    device = fast_device(n_row, n_col) if (n_row, n_col) == (len(RING), 2 * len(RING)) else general_device
    return jax.shard_map(device, mesh=mesh, in_specs=in_specs, out_specs=out_specs, check_vma=False)
```
